128 devices in a mesh: inner: 8 (over z, core), outer: 16 (over x, y).
Axes of the slice: x: 4, y: 4, z: 4, core: 2. Of those that a mesh axis runs over, the one named last changes fastest.
Arguments:
- inputs: bfloat16 [131072, 4096], P(('inner', 'outer')), may hold values from -6 to 6
- cotangent: bfloat16 [131072, 4096], P(('inner', 'outer')), may hold values from -0.176776695 to 0.176776695
- weights: bfloat16 [2, 64, 128, 128], replicated, may hold values from -0.375 to 0.375
- block_rows: int32 [2, 64], replicated, may hold values from 0 to 31, as said below
- block_cols: int32 [2, 64], replicated, may hold values from 0 to 31, as said below
- momentum: float32 [2, 8192, 128], P(None, ('inner', 'outer')), may hold values from -6 to 6
Outputs:
- new_weights: bfloat16 [2, 8192, 128], P(None, ('inner', 'outer'))
- new_momentum: float32 [2, 8192, 128], P(None, ('inner', 'outer'))
The draws below stay inside these ranges and needn't reach their ends.
Inputs may be any that keep to these rules, and one draw needn't show every extreme that they name: For each p the 64 pairs (block_rows[p, n], block_cols[p, n]) are distinct. `block_cols`: see block_rows.
All inputs are finite; a program needn't handle non-finite values.
Results may differ from the reference program's by a relative error of at most 0.01.
Values may be sent and summed in bfloat16 or wider, within the bound.
A program may use at most 320 MiB of HBM per device.

```python
import jax
import jax.numpy as jnp
from jax import lax

D = 4096
BLK = 128
TOK_DEV = 1024
NCB = 32
NB = 64
OWN = 8
TOKENS = 131072
N_INNER = 8
N_OUTER = 16


def pattern_pair(key):
    pattern_key = jax.random.fold_in(key, 7)
    rows_list = []
    cols_list = []
    for projection in range(2):
        shuffled = jax.random.permutation(jax.random.fold_in(pattern_key, projection), NCB * NCB)[:NB]
        rows_list.append((shuffled // NCB).astype(jnp.int32))
        cols_list.append((shuffled % NCB).astype(jnp.int32))
    return (jnp.stack(rows_list), jnp.stack(cols_list))


def draw_block_rows(key, part):
    return pattern_pair(key)[0]


def draw_block_cols(key, part):
    return pattern_pair(key)[1]


def draw_inputs(key, part):
    mean_key, noise_key = jax.random.split(key)
    feature_mean = jax.random.truncated_normal(mean_key, -4.0, 4.0, (D,), jnp.float32)
    noise_part = jax.random.truncated_normal(noise_key, -4.0, 4.0, (TOKENS, D), jnp.float32)
    feature_mean = 0.5 * feature_mean
    return (feature_mean[None, :] + noise_part).astype(jnp.bfloat16)


def draw_cotangent(key, part):
    mean_key, noise_key = jax.random.split(key)
    feature_mean = jax.random.truncated_normal(mean_key, -4.0, 4.0, (D,), jnp.float32)
    noise_part = jax.random.truncated_normal(noise_key, -4.0, 4.0, (TOKENS, D), jnp.float32)
    device_order = (jnp.arange(TOKENS, dtype=jnp.int32) // TOK_DEV).astype(jnp.float32)
    device_rate = 3.0 ** (device_order / (N_INNER * N_OUTER - 1.0))
    scaled = device_rate[:, None] * (0.3 * feature_mean[None, :] + noise_part) * (TOK_DEV * N_INNER) ** (-0.5)
    return scaled.astype(jnp.bfloat16)


def level_of(own_key, dims, cuts, least, high):
    def one(position, blocks):
        steps = jax.random.uniform(jax.random.fold_in(jax.random.fold_in(own_key, 6), position), (blocks,), jnp.float32, least / len(cuts), high / len(cuts))
        return jnp.repeat(jnp.exp(steps), dims[position] // blocks).reshape((-1,) + (1,) * (len(dims) - position - 1))

    factor_of = one(*cuts[0])
    for cut in cuts[1:]:
        factor_of = factor_of * one(*cut)
    return factor_of


def normal_values(rng, shape, deviation, reach, cuts=(), held_as=jnp.bfloat16):
    values = deviation * jax.random.normal(rng, shape, jnp.float32)
    if cuts:
        values = values * level_of(rng, shape, cuts, -0.22, 0.18)
    return jnp.clip(values, -reach, reach).astype(held_as)


def setup_inputs(seed: int = 0) -> dict:
    streams_of = jax.random.split(jax.random.key(seed), 7)
    return {
        "inputs": draw_inputs(jax.random.fold_in(streams_of[6], 71), 0),
        "cotangent": draw_cotangent(jax.random.fold_in(streams_of[6], 71), 0),
        "weights": normal_values(streams_of[2], (2, NB, BLK, BLK), (NB * BLK // NCB) ** -0.5, 0.375),
        "block_rows": draw_block_rows(jax.random.fold_in(streams_of[6], 71), 0),
        "block_cols": draw_block_cols(jax.random.fold_in(streams_of[6], 71), 0),
        "momentum": normal_values(streams_of[5], (2, NB * BLK, BLK), 1.0, 6.0, ((1, 128),), jnp.float32),
    }


dot_epsilon = 1e-6
momentum_decay = 0.9
step_rate = 0.05
root_half = 0.7071067811865476
inv_root_tau = 0.3989422804014327


def selector(indices, total_count):
    return (indices[..., None] == jnp.arange(total_count, dtype=jnp.int32)).astype(jnp.float32)


def device_terms(tokens_local, cot_local, weights, block_rows, block_cols):
    rows_here = tokens_local.shape[0]
    block_size = weights.shape[2]
    column_blocks = tokens_local.shape[1] // block_size
    row_select = selector(block_rows, column_blocks)
    col_select = selector(block_cols, column_blocks)
    weights_wide = weights.astype(jnp.float32)
    token_blocks = jnp.take(tokens_local.reshape(rows_here, column_blocks, block_size), block_rows[0], axis=1).astype(jnp.float32)
    first_terms = jnp.einsum('tnk,nkj->tnj', token_blocks, weights_wide[0], precision=lax.Precision.HIGHEST)
    hidden = jnp.einsum('tnj,nc->tcj', first_terms, col_select[0], precision=lax.Precision.HIGHEST)
    cumulative = 0.5 * (1.0 + jax.scipy.special.erf(hidden * root_half))
    activated = (hidden * cumulative).astype(jnp.bfloat16)
    gelu_slope = cumulative + hidden * jnp.exp(-0.5 * hidden * hidden) * inv_root_tau
    cot_blocks = jnp.take(cot_local.reshape(rows_here, column_blocks, block_size), block_cols[1], axis=1).astype(jnp.float32)
    back_terms = jnp.einsum('tnj,nkj->tnk', cot_blocks, weights_wide[1], precision=lax.Precision.HIGHEST)
    grad_act = jnp.einsum('tnk,nc->tck', back_terms, row_select[1], precision=lax.Precision.HIGHEST)
    grad_hidden = (grad_act * gelu_slope).astype(jnp.bfloat16)
    act_blocks = jnp.take(activated, block_rows[1], axis=1).astype(jnp.float32)
    second_grad = jnp.einsum('tnk,tnj->nkj', act_blocks, cot_blocks, precision=lax.Precision.HIGHEST)
    hid_blocks = jnp.take(grad_hidden, block_cols[0], axis=1).astype(jnp.float32)
    first_grad = jnp.einsum('tnk,tnj->nkj', token_blocks, hid_blocks, precision=lax.Precision.HIGHEST)
    return jnp.stack([first_grad, second_grad]).astype(jnp.bfloat16)


def reference(inputs, cotangent, weights, block_rows, block_cols, momentum):
    tokens_grid = inputs.reshape(N_INNER, N_OUTER, TOK_DEV, D)
    cot_grid = cotangent.reshape(N_INNER, N_OUTER, TOK_DEV, D)

    def outer_sum(outer_index):
        def one_device(inner_index):
            return device_terms(tokens_grid[inner_index, outer_index], cot_grid[inner_index, outer_index], weights, block_rows, block_cols)

        terms = lax.map(one_device, jnp.arange(N_INNER, dtype=jnp.int32))
        terms = lax.optimization_barrier(terms)
        return jnp.sum(terms.astype(jnp.float32), axis=0)

    summed = lax.map(outer_sum, jnp.arange(N_OUTER, dtype=jnp.int32))
    vectors = summed.reshape(N_OUTER, 2, N_INNER, OWN * BLK * BLK)
    levels = N_OUTER.bit_length() - 1
    for level_bit in range(levels):
        paired = vectors.reshape((vectors.shape[0] // 2, 2) + vectors.shape[1:])
        lower_part = paired[:, 0]
        upper_part = paired[:, 1]
        cross = jnp.sum(lower_part * upper_part, axis=-1, keepdims=True)
        lower_norm = jnp.sum(lower_part * lower_part, axis=-1, keepdims=True)
        upper_norm = jnp.sum(upper_part * upper_part, axis=-1, keepdims=True)
        vectors = (1.0 - cross / (2.0 * (lower_norm + dot_epsilon))) * lower_part + (1.0 - cross / (2.0 * (upper_norm + dot_epsilon))) * upper_part
    combined = vectors[0].reshape(2, NB * BLK, BLK)
    new_momentum = momentum_decay * momentum + combined
    new_weights = (weights.reshape(2, NB * BLK, BLK).astype(jnp.float32) - step_rate * new_momentum).astype(jnp.bfloat16)
    return new_weights, new_momentum
```

```python
import functools
import jax
import jax.numpy as jnp
from jax import lax
from jax.sharding import PartitionSpec as P
from jax.experimental import pallas as pl
from jax.experimental.pallas import tpu as pltpu
f32 = jnp.float32
bf = jnp.bfloat16
i32 = jnp.int32
dot_epsilon = 1e-06
momentum_decay = 0.9
step_rate = 0.05
NCB = 32
OWN = 8
ZS = 4
NOUT = 16
PIECE = 64
root_half = 0.7071067811865476
inv_root_tau = 0.3989422804014327

def forward_kernel(sub, rows_ref, cols_ref, x_ref, cot_ref, w_ref, act_ref, gh_ref, head, link, extra_h, extra_a):
    blk=w_ref.shape[2]; nb=w_ref.shape[1]; ncb=x_ref.shape[1]//blk; tile=x_ref.shape[0]
    @pl.when(pl.program_id(0)==0)
    def _():
        extra_h[...]=jnp.zeros_like(extra_h); extra_a[...]=jnp.zeros_like(extra_a)
        def clear(c,_):
            head[0,c]=nb; head[1,c]=nb
            return 0
        lax.fori_loop(0,ncb,clear,0)
        link[0,nb]=nb; link[1,nb]=nb
        def push(n,_):
            c=cols_ref[0,n]; link[0,n]=head[0,c]; head[0,c]=n
            r=rows_ref[1,n]; link[1,n]=head[1,r]; head[1,r]=n
            return 0
        lax.fori_loop(0,nb,push,0)
    def take(p,n):
        safe=jnp.minimum(n,nb-1)
        w=w_ref[p,safe]
        w=jnp.where(n<nb,w,jnp.zeros_like(w))
        feat=rows_ref[0,safe] if p==0 else cols_ref[1,safe]
        return w, pl.ds(pl.multiple_of(feat*blk,blk),blk)
    def pair(p,n,m):
        w1,d1=take(p,n); w2,d2=take(p,m)
        return jnp.concatenate([w1,w2],axis=p), d1, d2
    def product(p,prepared,rows):
        w,d1,d2=prepared
        ref=x_ref if p==0 else cot_ref
        left=jnp.concatenate([ref[rows,d1],ref[rows,d2]],axis=1)
        dims=(((1,),(p,)),((),()))
        return lax.dot_general(left,w,dims,preferred_element_type=f32)
    def column(c,_):
        a0=head[0,c]; b0=link[0,a0]; m0=link[0,b0]
        a1=head[1,c]; b1=link[1,a1]; m1=link[1,b1]
        for p,first,store in ((0,m0,extra_h),(1,m1,extra_a)):
            def more(n,p=p,store=store):
                second=link[p,n]
                got=pair(p,n,second)
                for s in range(0,tile,sub):
                    rows=pl.ds(s,sub)
                    store[rows,:]+=product(p,got,rows)
                return link[p,second]
            lax.while_loop(lambda n: n<nb, more, first)
        got0=pair(0,a0,b0); got1=pair(1,a1,b1)
        for s in range(0,tile,sub):
            rows=pl.ds(s,sub)
            h=product(0,got0,rows)+extra_h[rows,:]
            g=product(1,got1,rows)+extra_a[rows,:]
            cum=0.5*(1.0+lax.erf(h*root_half))
            act_ref[c,rows,:]=(h*cum).astype(bf)
            slope=cum+h*jnp.exp(-0.5*h*h)*inv_root_tau
            gh_ref[c,rows,:]=(g*slope).astype(bf)
        @pl.when(m0<nb)
        def _(): extra_h[...]=jnp.zeros_like(extra_h)
        @pl.when(m1<nb)
        def _(): extra_a[...]=jnp.zeros_like(extra_a)
        return 0
    lax.fori_loop(0,ncb,column,0)

def forward(inputs,cotangent,weights,block_rows,block_cols,tile=512,sub=128):
    T,D=inputs.shape
    nb=weights.shape[1]; ncb=D//weights.shape[2]; blk=weights.shape[2]
    smem=pl.BlockSpec(memory_space=pltpu.SMEM)
    wide=pl.BlockSpec((tile,D),lambda t:(t,0))
    return pl.pallas_call(functools.partial(forward_kernel,sub),
        grid=(T//tile,),
        in_specs=[smem,smem,wide,wide,pl.BlockSpec(weights.shape,lambda t:(0,0,0,0),pipeline_mode=pl.Buffered(1))],
        out_specs=[pl.BlockSpec((ncb,tile,blk),lambda t:(0,t,0))]*2,
        out_shape=[jax.ShapeDtypeStruct((ncb,T,blk),bf)]*2,
        scratch_shapes=[pltpu.SMEM((2,ncb),i32),pltpu.SMEM((2,nb+1),i32),pltpu.VMEM((tile,blk),f32),pltpu.VMEM((tile,blk),f32)],
        compiler_params=pltpu.CompilerParams(vmem_limit_bytes=60*2**20),
        name="forward",
    )(block_rows,block_cols,inputs,cotangent,weights)


def combine_kernel(rows_ref, cols_ref, x_hbm, cot_hbm, act_hbm, gh_hbm, w_hbm, mom_ref, outw_ref, outm_ref,
                   x_v, cot_v, act_v, gh_v, w_v, psend, own, precv, zsend, mid, fin, vsend, pieces, wide, gsend, grecv,
                   load_sem, w_sem, keep_sem, psend_sem, precv_sem, zsend_sem, mid_sem, fin_sem, vsend_sem, vrecv_sem, gsend_sem, grecv_sem):
    MESH = pl.DeviceIdType.MESH
    blk = x_v.shape[2]
    inner = lax.axis_index("inner")
    outer = lax.axis_index("outer")
    z = inner // 2
    core = lax.rem(inner, 2)
    other = 1 - core
    up = {"inner": lax.rem(z + 1, ZS) * 2 + core}
    down = {"inner": lax.rem(z + ZS - 1, ZS) * 2 + core}
    mate = {"inner": z * 2 + other}

    def load_wide(src, dst, sem):
        for c in range(NCB):
            pltpu.make_async_copy(src.at[:, c * blk:(c + 1) * blk], dst.at[c], sem).start()

    pltpu.make_async_copy(act_hbm, act_v, load_sem.at[0]).start()
    load_wide(cot_hbm, cot_v, load_sem.at[1])
    w_copy = pltpu.make_async_copy(
        w_hbm.at[:, inner * OWN + outer // 2, pl.ds(lax.rem(outer, 2) * PIECE, PIECE), :], w_v, w_sem)
    w_copy.start()

    barrier = pltpu.get_barrier_semaphore()
    for peer in (up, down, mate):
        pl.semaphore_signal(barrier, inc=1, device_id=peer, device_id_type=MESH)
    for k in range(1, NOUT):
        pl.semaphore_signal(barrier, inc=1, device_id={"outer": lax.rem(outer + k, NOUT)}, device_id_type=MESH)
    pl.semaphore_wait(barrier, 3 + NOUT - 1)

    pltpu.make_async_copy(act_hbm, act_v, load_sem.at[0]).wait()
    pltpu.make_async_copy(act_hbm, cot_v, load_sem.at[1]).wait()
    pltpu.make_async_copy(gh_hbm, gh_v, load_sem.at[2]).start()
    load_wide(x_hbm, x_v, load_sem.at[3])

    def mate_copy(g):
        return pltpu.make_async_remote_copy(src_ref=psend.at[g], dst_ref=precv.at[g], send_sem=psend_sem.at[g],
                                            recv_sem=precv_sem.at[g], device_id=mate, device_id_type=MESH)

    def z_copy(q, slot):
        dst, sem = ((mid, mid_sem), (mid, mid_sem), (fin, fin_sem), (fin, fin_sem), (fin, fin_sem), (fin, fin_sem))[slot]
        k = (0, 1, 3, 1, 0, 2)[slot]
        peer = up if slot in (0, 2, 4) else down
        return pltpu.make_async_remote_copy(src_ref=zsend.at[q, slot], dst_ref=dst.at[q, k], send_sem=zsend_sem.at[q, slot],
                                            recv_sem=sem.at[q, k], device_id=peer, device_id_type=MESH)

    def grads(q, block0, dst):
        def four(i, _):
            for u in range(4):
                m = i * 4 + u
                n = block0 + m
                r = rows_ref[1 - q, n]
                c = cols_ref[1 - q, n]
                left = act_v[r] if q == 0 else x_v[r]
                right = cot_v[c] if q == 0 else gh_v[c]
                dst[m] = lax.dot_general(left, right, (((0,), (0,)), ((), ())),
                                         preferred_element_type=jnp.float32).astype(jnp.bfloat16)
            return 0
        lax.fori_loop(0, OWN // 4, four, 0)

    HALF = OWN // 2
    def chip(g, lo):
        part = slice(lo, lo + HALF)
        return own[g, part].astype(jnp.float32) + precv[g, part].astype(jnp.float32)

    def send_z(q, slot, value):
        zsend[q, slot] = value.astype(jnp.bfloat16)
        z_copy(q, slot).start()

    def process(q, d):
        g = q * ZS + d
        mate_copy(g).wait_recv()
        if d == 0:
            send_z(q, 0, chip(g, 0))
            send_z(q, 1, chip(g, HALF))
        elif d == 1:
            send_z(q, 2, chip(g, HALF))
        elif d == 2:
            send_z(q, 3, chip(g, 0))
        else:
            z_copy(q, 0).wait_recv()
            send_z(q, 4, chip(q * ZS + 1, 0) + mid[q, 0].astype(jnp.float32))
            z_copy(q, 1).wait_recv()
            send_z(q, 5, chip(q * ZS + 2, HALF) + mid[q, 1].astype(jnp.float32))

    def v_copy(q, k):
        to = lax.rem(outer + k, NOUT)
        return pltpu.make_async_remote_copy(src_ref=vsend.at[q, to], dst_ref=pieces.at[q, k], send_sem=vsend_sem.at[q, k],
                                            recv_sem=vrecv_sem.at[q, k], device_id={"outer": to}, device_id_type=MESH)

    def finish(q):
        for slot in (2, 3, 4, 5):
            z_copy(q, slot).wait_recv()
        g = q * ZS + 3
        for part in range(2):
            total = chip(g, part * HALF) + fin[q, 2 * part].astype(jnp.float32) + fin[q, 2 * part + 1].astype(jnp.float32)
            vsend[q, part * (NOUT // 2):(part + 1) * (NOUT // 2)] = total.astype(jnp.bfloat16).reshape(NOUT // 2, PIECE, blk)
        for k in range(1, NOUT):
            v_copy(q, k).start()
        keep = pltpu.make_async_copy(vsend.at[q, outer], pieces.at[q, 0], keep_sem.at[q])
        keep.start()

    for q in range(2):
        if q == 1:
            pltpu.make_async_copy(gh_hbm, gh_v, load_sem.at[2]).wait()
            pltpu.make_async_copy(gh_hbm, x_v, load_sem.at[3]).wait()
        for d in range(ZS):
            g = q * ZS + d
            owner = lax.rem(z + (2, 1, 3, 0)[d], ZS) * 2
            grads(q, (owner + other) * OWN, psend.at[g])
            mate_copy(g).start()
            grads(q, (owner + core) * OWN, own.at[g])
            if g > 0:
                process((g - 1) // ZS, (g - 1) % ZS)
    process(1, 3)
    finish(0)
    finish(1)

    def gram(q):
        for k in range(1, NOUT):
            v_copy(q, k).wait_recv()
        pltpu.make_async_copy(vsend.at[q, outer], pieces.at[q, 0], keep_sem.at[q]).wait()
        for s in range(NOUT):
            wide[q, s * PIECE:(s + 1) * PIECE] = pieces[q, lax.rem(outer - s + NOUT, NOUT)].astype(jnp.float32)
        picked = [wide[q, pl.ds(r, NOUT, stride=PIECE), :].astype(jnp.bfloat16) for r in range(PIECE)]
        flat = jnp.concatenate(picked, axis=1)
        return lax.dot_general(flat, flat, (((1,), (1,)), ((), ())), preferred_element_type=jnp.float32)

    g0 = gram(0)
    g1 = gram(1)
    gsend[...] = jnp.concatenate([g0, g1, jnp.zeros((NOUT, blk - 2 * NOUT), jnp.float32)], axis=1)

    def g_copy(k):
        to = lax.rem(outer + k, NOUT)
        return pltpu.make_async_remote_copy(src_ref=gsend, dst_ref=grecv.at[k - 1], send_sem=gsend_sem.at[k - 1],
                                            recv_sem=grecv_sem.at[k - 1], device_id={"outer": to}, device_id_type=MESH)
    for k in range(1, NOUT):
        g_copy(k).start()
    w_copy.wait()
    total = gsend[...]
    for k in range(1, NOUT):
        g_copy(k).wait_recv()
        total = total + grecv[k - 1]

    row = lax.broadcasted_iota(jnp.int32, (NOUT, NOUT), 0)
    lane = lax.broadcasted_iota(jnp.int32, (NOUT, NOUT), 1)
    for q in range(2):
        q_mat = total[:, q * NOUT:(q + 1) * NOUT]
        coef = jnp.ones((NOUT, 1), jnp.float32)
        step = 1
        while step < NOUT:
            same = row == lane
            pair = (row ^ step) == lane
            def mult(axis):
                norm = jnp.maximum(jnp.sum(jnp.where(same, q_mat, 0.0), axis=axis, keepdims=True), 0.0)
                cross = jnp.sum(jnp.where(pair, q_mat, 0.0), axis=axis, keepdims=True)
                return 1.0 - cross / (2.0 * (norm + dot_epsilon))
            mc, mr = mult(1), mult(0)
            coef = coef * mc
            q_mat = q_mat * mc * mr
            def partner(m, axis):
                parts = []
                for i in range(NOUT):
                    j = i ^ step
                    parts.append(m[j:j + 1, :] if axis == 0 else m[:, j:j + 1])
                return jnp.concatenate(parts, axis=axis)
            q_mat = q_mat + partner(q_mat, 0)
            q_mat = q_mat + partner(q_mat, 1)
            step *= 2
        comb = jnp.zeros((PIECE, blk), jnp.float32)
        for s in range(NOUT):
            comb = comb + coef[s:s + 1, :] * wide[q, s * PIECE:(s + 1) * PIECE]
        p = 1 - q
        new_m = momentum_decay * mom_ref[p] + comb
        outm_ref[p] = new_m
        outw_ref[p] = (w_v[p].astype(jnp.float32) - step_rate * new_m).astype(jnp.bfloat16)

    for g in range(2 * ZS):
        mate_copy(g).wait_send()
    for q in range(2):
        for slot in range(6):
            z_copy(q, slot).wait_send()
        for k in range(1, NOUT):
            v_copy(q, k).wait_send()
    for k in range(1, NOUT):
        g_copy(k).wait_send()


def combine(inputs, cotangent, activated, grad_hidden, weights, block_rows, block_cols, momentum):
    T = inputs.shape[0]
    blk = weights.shape[2]
    bf, f32 = jnp.bfloat16, jnp.float32
    smem = pl.BlockSpec(memory_space=pltpu.SMEM)
    hbm = pl.BlockSpec(memory_space=pl.ANY)
    vmem = pl.BlockSpec(memory_space=pltpu.VMEM)
    dma = pltpu.SemaphoreType.DMA
    V = pltpu.VMEM
    return pl.pallas_call(
        combine_kernel,
        in_specs=[smem, smem, hbm, hbm, hbm, hbm, hbm, vmem],
        out_specs=[vmem, vmem],
        out_shape=[jax.ShapeDtypeStruct(momentum.shape, bf), jax.ShapeDtypeStruct(momentum.shape, f32)],
        scratch_shapes=[
            V((NCB, T, blk), bf), V((NCB, T, blk), bf), V((NCB, T, blk), bf), V((NCB, T, blk), bf), V((2, PIECE, blk), bf),
            V((2 * ZS, OWN, blk, blk), bf), V((2 * ZS, OWN, blk, blk), bf), V((2 * ZS, OWN, blk, blk), bf),
            V((2, 6, OWN // 2, blk, blk), bf), V((2, 2, OWN // 2, blk, blk), bf), V((2, 4, OWN // 2, blk, blk), bf),
            V((2, NOUT, PIECE, blk), bf), V((2, NOUT, PIECE, blk), bf), V((2, NOUT * PIECE, blk), f32),
            V((NOUT, blk), f32), V((NOUT - 1, NOUT, blk), f32),
            dma((4,)), dma, dma((2,)), dma((2 * ZS,)), dma((2 * ZS,)), dma((2, 6)), dma((2, 2)), dma((2, 4)),
            dma((2, NOUT)), dma((2, NOUT)), dma((NOUT - 1,)), dma((NOUT - 1,)),
        ],
        compiler_params=pltpu.CompilerParams(vmem_limit_bytes=62 * 2**20, collective_id=0, has_side_effects=True),
        name="combine",
    )(block_rows, block_cols, inputs, cotangent, activated, grad_hidden, weights, momentum)


def local(inputs, cotangent, weights, block_rows, block_cols, momentum):
    activated, grad_hidden = forward(inputs, cotangent, weights, block_rows, block_cols)
    return tuple(combine(inputs, cotangent, activated, grad_hidden, weights, block_rows, block_cols, momentum))


def solution(mesh):
    return jax.shard_map(
        local,
        mesh=mesh,
        in_specs=(
            P(("inner", "outer"), None),
            P(("inner", "outer"), None),
            P(),
            P(),
            P(),
            P(None, ("inner", "outer"), None),
        ),
        out_specs=(P(None, ("inner", "outer"), None), P(None, ("inner", "outer"), None)),
        check_vma=False,
    )
```

```python
import functools
import jax
import jax.numpy as jnp
from jax import lax
from jax.sharding import PartitionSpec as P
from jax.experimental import pallas as pl
from jax.experimental.pallas import tpu as pltpu
f32 = jnp.float32
bf = jnp.bfloat16
i32 = jnp.int32
dot_epsilon = 1e-06
momentum_decay = 0.9
step_rate = 0.05
NCB = 32
OWN = 8
ZS = 4
NOUT = 16
PIECE = 64
root_half = 0.7071067811865476
inv_root_tau = 0.3989422804014327

def forward_kernel(sub, rows_ref, cols_ref, x_hbm, cot_hbm, w_hbm, x_ref, cot_ref, act_ref, gh_ref,
                   head, link, seen, w_ref, extra_h, extra_a, sem, w_sem):
    blk = w_ref.shape[2]
    nb = w_ref.shape[1]
    tokens = x_ref.shape[1]

    w_loads = [pltpu.make_async_copy(w_hbm.at[p], w_ref.at[p], w_sem.at[p]) for p in range(2)]
    for load in w_loads:
        load.start()

    def clear(c, _):
        for p in range(2):
            head[p, c] = nb
            seen[p, c] = 0
        return 0
    lax.fori_loop(0, NCB, clear, 0)
    link[0, nb] = nb
    link[1, nb] = nb

    def push(n, _):
        c = cols_ref[0, n]
        link[0, n] = head[0, c]
        head[0, c] = n
        r = rows_ref[1, n]
        link[1, n] = head[1, r]
        head[1, r] = n
        return 0
    lax.fori_loop(0, nb, push, 0)

    def feature(p, n):
        return rows_ref[0, n] if p == 0 else cols_ref[1, n]

    def copy(p, f):
        src, dst = ((x_hbm, x_ref), (cot_hbm, cot_ref))[p]
        return pltpu.make_async_copy(src.at[:, pl.ds(pl.multiple_of(f * blk, blk), blk)], dst.at[f], sem.at[p, f])

    def fetch(c, _):
        for p in range(2):
            def one(n, p=p):
                f = feature(p, n)
                @pl.when(seen[p, f] == 0)
                def _():
                    seen[p, f] = 1
                    copy(p, f).start()
                return link[p, n]
            lax.while_loop(lambda n: n < nb, one, head[p, c])
        return 0
    lax.fori_loop(0, NCB, fetch, 0)
    for load in w_loads:
        load.wait()

    def arrive(p, f):
        @pl.when(seen[p, f] == 1)
        def _():
            seen[p, f] = 2
            copy(p, f).wait()

    def take(p, n):
        safe = jnp.minimum(n, nb - 1)
        w = w_ref[p, safe]
        return jnp.where(n < nb, w, jnp.zeros_like(w)), feature(p, safe)

    def pair(p, n, m):
        w1, f1 = take(p, n)
        w2, f2 = take(p, m)
        f2 = jnp.where(m < nb, f2, f1)
        return jnp.concatenate([w1, w2], axis=p), f1, f2

    def product(p, got, rows):
        w, f1, f2 = got
        ref = x_ref if p == 0 else cot_ref
        left = jnp.concatenate([ref[f1, rows, :], ref[f2, rows, :]], axis=1)
        return lax.dot_general(left, w, (((1,), (p,)), ((), ())), preferred_element_type=f32)

    def column(c, _):
        firsts, seconds, rests = [], [], []
        for p in range(2):
            def one(n, p=p):
                arrive(p, feature(p, n))
                return link[p, n]
            lax.while_loop(lambda n: n < nb, one, head[p, c])
            a = head[p, c]
            b = link[p, a]
            d = link[p, b]
            e = link[p, d]
            firsts.append((a, b))
            seconds.append((d, e))
            rests.append(link[p, e])
        @pl.when((firsts[0][0] == nb) | (firsts[1][0] == nb))
        def _():
            for p in range(2):
                arrive(p, feature(p, nb - 1))
        more = jnp.logical_or(rests[0] < nb, rests[1] < nb)
        two = [jnp.logical_or(seconds[p][0] < nb, more) for p in range(2)]

        def body(n0, n1, extra):
            gots = []
            for p, count in ((0, n0), (1, n1)):
                gots.append([pair(p, *firsts[p])] + ([pair(p, *seconds[p])] if count == 2 else []))
            for s in range(0, tokens, sub):
                rows = pl.ds(s, sub)
                h, g = (sum(product(p, got, rows) for got in gots[p]) for p in range(2))
                if extra:
                    h = h + extra_h[rows, :]
                    g = g + extra_a[rows, :]
                cum = 0.5 * (1.0 + lax.erf(h * root_half))
                act_ref[c, rows, :] = (h * cum).astype(bf)
                slope = cum + h * jnp.exp(-0.5 * h * h) * inv_root_tau
                gh_ref[c, rows, :] = (g * slope).astype(bf)

        for n0 in (1, 2):
            for n1 in (1, 2):
                @pl.when(jnp.logical_not(more) & (two[0] == (n0 == 2)) & (two[1] == (n1 == 2)))
                def _(n0=n0, n1=n1):
                    body(n0, n1, False)

        @pl.when(more)
        def _():
            for p, store in ((0, extra_h), (1, extra_a)):
                store[...] = jnp.zeros_like(store)
                def add(n, p=p, store=store):
                    m = link[p, n]
                    got = pair(p, n, m)
                    for s in range(0, tokens, sub):
                        store[pl.ds(s, sub), :] += product(p, got, pl.ds(s, sub))
                    return link[p, m]
                lax.while_loop(lambda n: n < nb, add, rests[p])
            body(2, 2, True)
        return 0
    lax.fori_loop(0, NCB, column, 0)


def forward(inputs, cotangent, weights, block_rows, block_cols, sub=256):
    T = inputs.shape[0]
    blk = weights.shape[2]
    nb = weights.shape[1]
    smem = pl.BlockSpec(memory_space=pltpu.SMEM)
    hbm = pl.BlockSpec(memory_space=pltpu.HBM)
    vmem = pl.BlockSpec(memory_space=pltpu.VMEM)
    return pl.pallas_call(
        functools.partial(forward_kernel, sub),
        in_specs=[smem, smem, hbm, hbm, hbm],
        out_specs=[vmem] * 4,
        out_shape=[pltpu.VMEM((NCB, T, blk), bf)] * 4,
        scratch_shapes=[
            pltpu.SMEM((2, NCB), jnp.int32), pltpu.SMEM((2, nb + 1), jnp.int32), pltpu.SMEM((2, NCB), jnp.int32),
            pltpu.VMEM(weights.shape, bf), pltpu.VMEM((T, blk), f32), pltpu.VMEM((T, blk), f32), pltpu.SemaphoreType.DMA((2, NCB)),
            pltpu.SemaphoreType.DMA((2,)),
        ],
        compiler_params=pltpu.CompilerParams(vmem_limit_bytes=26 * 2**20),
        name="forward",
    )(block_rows, block_cols, inputs, cotangent, weights)


def combine_kernel(rows_ref, cols_ref, x_v, cot_v, act_v, gh_v, out_ref,
                   psend, own, precv, zsend, mid, fin, vsend, pieces, wide, gsend, grecv,
                   keep_sem, psend_sem, precv_sem, zsend_sem, mid_sem, fin_sem, vsend_sem, vrecv_sem, gsend_sem, grecv_sem):
    MESH = pl.DeviceIdType.MESH
    blk = x_v.shape[2]
    inner = lax.axis_index("inner")
    outer = lax.axis_index("outer")
    z = inner // 2
    core = lax.rem(inner, 2)
    other = 1 - core
    up = {"inner": lax.rem(z + 1, ZS) * 2 + core}
    down = {"inner": lax.rem(z + ZS - 1, ZS) * 2 + core}
    mate = {"inner": z * 2 + other}

    barrier = pltpu.get_barrier_semaphore()
    for peer in (up, down, mate):
        pl.semaphore_signal(barrier, inc=1, device_id=peer, device_id_type=MESH)
    for k in range(1, NOUT):
        pl.semaphore_signal(barrier, inc=1, device_id={"outer": lax.rem(outer + k, NOUT)}, device_id_type=MESH)

    def mate_copy(g):
        return pltpu.make_async_remote_copy(src_ref=psend.at[g], dst_ref=precv.at[g], send_sem=psend_sem.at[g],
                                            recv_sem=precv_sem.at[g], device_id=mate, device_id_type=MESH)

    def z_copy(q, slot):
        dst, sem = ((mid, mid_sem), (mid, mid_sem), (fin, fin_sem), (fin, fin_sem), (fin, fin_sem), (fin, fin_sem))[slot]
        k = (0, 1, 3, 1, 0, 2)[slot]
        peer = up if slot in (0, 2, 4) else down
        return pltpu.make_async_remote_copy(src_ref=zsend.at[q, slot], dst_ref=dst.at[q, k], send_sem=zsend_sem.at[q, slot],
                                            recv_sem=sem.at[q, k], device_id=peer, device_id_type=MESH)

    def grads(q, block0, dst):
        def four(i, _):
            for u in range(4):
                m = i * 4 + u
                n = block0 + m
                r = rows_ref[1 - q, n]
                c = cols_ref[1 - q, n]
                left = act_v[r] if q == 0 else x_v[r]
                right = cot_v[c] if q == 0 else gh_v[c]
                dst[m] = lax.dot_general(left, right, (((0,), (0,)), ((), ())),
                                         preferred_element_type=f32).astype(bf)
            return 0
        lax.fori_loop(0, OWN // 4, four, 0)

    HALF = OWN // 2
    def chip(g, lo):
        part = slice(lo, lo + HALF)
        return own[g, part].astype(f32) + precv[g, part].astype(f32)

    def send_z(q, slot, value):
        zsend[q, slot] = value.astype(bf)
        z_copy(q, slot).start()

    def process(q, d):
        g = q * ZS + d
        mate_copy(g).wait_recv()
        if d == 0:
            send_z(q, 0, chip(g, 0))
            send_z(q, 1, chip(g, HALF))
        elif d == 1:
            send_z(q, 2, chip(g, HALF))
        elif d == 2:
            send_z(q, 3, chip(g, 0))
        else:
            z_copy(q, 0).wait_recv()
            send_z(q, 4, chip(q * ZS + 1, 0) + mid[q, 0].astype(f32))
            z_copy(q, 1).wait_recv()
            send_z(q, 5, chip(q * ZS + 2, HALF) + mid[q, 1].astype(f32))

    def v_copy(q, k):
        to = lax.rem(outer + k, NOUT)
        return pltpu.make_async_remote_copy(src_ref=vsend.at[q, to], dst_ref=pieces.at[q, k], send_sem=vsend_sem.at[q, k],
                                            recv_sem=vrecv_sem.at[q, k], device_id={"outer": to}, device_id_type=MESH)

    def finish(q):
        for slot in (2, 3, 4, 5):
            z_copy(q, slot).wait_recv()
        g = q * ZS + 3
        for part in range(2):
            total = chip(g, part * HALF) + fin[q, 2 * part].astype(f32) + fin[q, 2 * part + 1].astype(f32)
            vsend[q, part * (NOUT // 2):(part + 1) * (NOUT // 2)] = total.astype(bf).reshape(NOUT // 2, PIECE, blk)
        for k in range(1, NOUT):
            v_copy(q, k).start()
        keep = pltpu.make_async_copy(vsend.at[q, outer], pieces.at[q, 0], keep_sem.at[q])
        keep.start()

    for q in range(2):
        for d in range(ZS):
            g = q * ZS + d
            owner = lax.rem(z + (2, 1, 3, 0)[d], ZS) * 2
            grads(q, (owner + other) * OWN, psend.at[g])
            if g == 0:
                pl.semaphore_wait(barrier, 3 + NOUT - 1)
            mate_copy(g).start()
            grads(q, (owner + core) * OWN, own.at[g])
            if g > 0:
                process((g - 1) // ZS, (g - 1) % ZS)
    process(1, 3)
    finish(0)
    finish(1)

    def gram(q):
        for k in range(1, NOUT):
            v_copy(q, k).wait_recv()
        pltpu.make_async_copy(vsend.at[q, outer], pieces.at[q, 0], keep_sem.at[q]).wait()
        for s in range(NOUT):
            wide[q, s * PIECE:(s + 1) * PIECE] = pieces[q, lax.rem(outer - s + NOUT, NOUT)].astype(f32)
        picked = [wide[q, pl.ds(r, NOUT, stride=PIECE), :].astype(bf) for r in range(PIECE)]
        flat = jnp.concatenate(picked, axis=1)
        return lax.dot_general(flat, flat, (((1,), (1,)), ((), ())), preferred_element_type=f32)

    g0 = gram(0)
    g1 = gram(1)
    gsend[...] = jnp.concatenate([g0, g1, jnp.zeros((NOUT, blk - 2 * NOUT), f32)], axis=1)

    def g_copy(k):
        to = lax.rem(outer + k, NOUT)
        return pltpu.make_async_remote_copy(src_ref=gsend, dst_ref=grecv.at[k - 1], send_sem=gsend_sem.at[k - 1],
                                            recv_sem=grecv_sem.at[k - 1], device_id={"outer": to}, device_id_type=MESH)
    for k in range(1, NOUT):
        g_copy(k).start()
    total = gsend[...]
    for k in range(1, NOUT):
        g_copy(k).wait_recv()
        total = total + grecv[k - 1]

    row = lax.broadcasted_iota(jnp.int32, (NOUT, NOUT), 0)
    lane = lax.broadcasted_iota(jnp.int32, (NOUT, NOUT), 1)
    for q in range(2):
        q_mat = total[:, q * NOUT:(q + 1) * NOUT]
        coef = jnp.ones((NOUT, 1), f32)
        step = 1
        while step < NOUT:
            same = row == lane
            pair = (row ^ step) == lane
            def mult(axis):
                norm = jnp.maximum(jnp.sum(jnp.where(same, q_mat, 0.0), axis=axis, keepdims=True), 0.0)
                cross = jnp.sum(jnp.where(pair, q_mat, 0.0), axis=axis, keepdims=True)
                return 1.0 - cross / (2.0 * (norm + dot_epsilon))
            mc, mr = mult(1), mult(0)
            coef = coef * mc
            q_mat = q_mat * mc * mr
            def partner(m, axis):
                parts = []
                for i in range(NOUT):
                    j = i ^ step
                    parts.append(m[j:j + 1, :] if axis == 0 else m[:, j:j + 1])
                return jnp.concatenate(parts, axis=axis)
            q_mat = q_mat + partner(q_mat, 0)
            q_mat = q_mat + partner(q_mat, 1)
            step *= 2
        comb = jnp.zeros((PIECE, blk), f32)
        for s in range(NOUT):
            comb = comb + coef[s:s + 1, :] * wide[q, s * PIECE:(s + 1) * PIECE]
        out_ref[1 - q] = comb

    for g in range(2 * ZS):
        mate_copy(g).wait_send()
    for q in range(2):
        for slot in range(6):
            z_copy(q, slot).wait_send()
        for k in range(1, NOUT):
            v_copy(q, k).wait_send()
    for k in range(1, NOUT):
        g_copy(k).wait_send()


def combine(tokens, cots, activated, grad_hidden, block_rows, block_cols):
    blk = tokens.shape[2]
    smem = pl.BlockSpec(memory_space=pltpu.SMEM)
    vmem = pl.BlockSpec(memory_space=pltpu.VMEM)
    dma = pltpu.SemaphoreType.DMA
    V = pltpu.VMEM
    return pl.pallas_call(
        combine_kernel,
        in_specs=[smem, smem, vmem, vmem, vmem, vmem],
        out_specs=vmem,
        out_shape=jax.ShapeDtypeStruct((2, PIECE, blk), f32),
        scratch_shapes=[
            V((2 * ZS, OWN, blk, blk), bf), V((2 * ZS, OWN, blk, blk), bf), V((2 * ZS, OWN, blk, blk), bf),
            V((2, 6, OWN // 2, blk, blk), bf), V((2, 2, OWN // 2, blk, blk), bf), V((2, 4, OWN // 2, blk, blk), bf),
            V((2, NOUT, PIECE, blk), bf), V((2, NOUT, PIECE, blk), bf), V((2, NOUT * PIECE, blk), f32),
            V((NOUT, blk), f32), V((NOUT - 1, NOUT, blk), f32),
            dma((2,)), dma((2 * ZS,)), dma((2 * ZS,)), dma((2, 6)), dma((2, 2)), dma((2, 4)),
            dma((2, NOUT)), dma((2, NOUT)), dma((NOUT - 1,)), dma((NOUT - 1,)),
        ],
        compiler_params=pltpu.CompilerParams(vmem_limit_bytes=16 * 2**20, collective_id=0, has_side_effects=True),
        name="combine",
    )(block_rows, block_cols, tokens, cots, activated, grad_hidden)


def local(inputs, cotangent, weights, block_rows, block_cols, momentum):
    parts = forward(inputs, cotangent, weights, block_rows, block_cols)
    combined = combine(*parts, block_rows, block_cols)
    new_momentum = momentum_decay * momentum + combined
    place = lax.axis_index("inner") * NOUT + lax.axis_index("outer")
    held = lax.dynamic_slice_in_dim(weights.reshape(2, -1, weights.shape[3]), place * PIECE, PIECE, 1)
    new_weights = (held.astype(f32) - step_rate * new_momentum).astype(bf)
    return new_weights, new_momentum


def solution(mesh):
    return jax.shard_map(
        local,
        mesh=mesh,
        in_specs=(
            P(("inner", "outer"), None),
            P(("inner", "outer"), None),
            P(),
            P(),
            P(),
            P(None, ("inner", "outer"), None),
        ),
        out_specs=(P(None, ("inner", "outer"), None), P(None, ("inner", "outer"), None)),
        check_vma=False,
    )
```

```python
import functools
import jax
import jax.numpy as jnp
from jax import lax
from jax.sharding import PartitionSpec as P
from jax.experimental import pallas as pl
from jax.experimental.pallas import tpu as pltpu
f32 = jnp.float32
bf = jnp.bfloat16
i32 = jnp.int32
dot_epsilon = 1e-06
momentum_decay = 0.9
step_rate = 0.05
NCB = 32
OWN = 8
ZS = 4
NOUT = 16
PIECE = 64
root_half = 0.7071067811865476
inv_root_tau = 0.3989422804014327

def forward_kernel(sub, rows_ref, cols_ref, x_hbm, cot_hbm, w_hbm, x_ref, cot_ref, act_ref, gh_ref,
                   head, link, seen, w_ref, extra_h, extra_a, sem, w_sem):
    blk = w_ref.shape[2]
    nb = w_ref.shape[1]
    tokens = x_ref.shape[1]

    w_loads = [pltpu.make_async_copy(w_hbm.at[p], w_ref.at[p], w_sem.at[p]) for p in range(2)]
    for load in w_loads:
        load.start()

    def clear(c, _):
        for p in range(2):
            head[p, c] = nb
            seen[p, c] = 0
        return 0
    lax.fori_loop(0, NCB, clear, 0, unroll=True)
    link[0, nb] = nb
    link[1, nb] = nb

    def push(n, _):
        c = cols_ref[0, n]
        link[0, n] = head[0, c]
        head[0, c] = n
        r = rows_ref[1, n]
        link[1, n] = head[1, r]
        head[1, r] = n
        return 0
    lax.fori_loop(0, nb, push, 0, unroll=8)

    def feature(p, n):
        return rows_ref[0, n] if p == 0 else cols_ref[1, n]

    def copy(p, f):
        src, dst = ((x_hbm, x_ref), (cot_hbm, cot_ref))[p]
        return pltpu.make_async_copy(src.at[:, pl.ds(pl.multiple_of(f * blk, blk), blk)], dst.at[f], sem.at[p, f])

    def fetch(c, _):
        for p in range(2):
            def one(n, p=p):
                f = feature(p, n)
                @pl.when(seen[p, f] == 0)
                def _():
                    seen[p, f] = 1
                    copy(p, f).start()
                return link[p, n]
            lax.while_loop(lambda n: n < nb, one, head[p, c])
        return 0
    lax.fori_loop(0, NCB, fetch, 0)
    for load in w_loads:
        load.wait()

    def arrive(p, f):
        @pl.when(seen[p, f] == 1)
        def _():
            seen[p, f] = 2
            copy(p, f).wait()

    def take(p, n):
        safe = jnp.minimum(n, nb - 1)
        w = w_ref[p, safe]
        return jnp.where(n < nb, w, jnp.zeros_like(w)), feature(p, safe)

    def pair(p, n, m):
        w1, f1 = take(p, n)
        w2, f2 = take(p, m)
        f2 = jnp.where(m < nb, f2, f1)
        return jnp.concatenate([w1, w2], axis=p), f1, f2

    def product(p, got, rows):
        w, f1, f2 = got
        ref = x_ref if p == 0 else cot_ref
        left = jnp.concatenate([ref[f1, rows, :], ref[f2, rows, :]], axis=1)
        return lax.dot_general(left, w, (((1,), (p,)), ((), ())), preferred_element_type=f32)

    def column(c, _):
        firsts, seconds, rests = [], [], []
        for p in range(2):
            def one(n, p=p):
                arrive(p, feature(p, n))
                return link[p, n]
            lax.while_loop(lambda n: n < nb, one, head[p, c])
            a = head[p, c]
            b = link[p, a]
            d = link[p, b]
            e = link[p, d]
            firsts.append((a, b))
            seconds.append((d, e))
            rests.append(link[p, e])
        @pl.when((firsts[0][0] == nb) | (firsts[1][0] == nb))
        def _():
            for p in range(2):
                arrive(p, feature(p, nb - 1))
        more = jnp.logical_or(rests[0] < nb, rests[1] < nb)
        two = [jnp.logical_or(seconds[p][0] < nb, more) for p in range(2)]

        def body(n0, n1, extra):
            gots = []
            for p, count in ((0, n0), (1, n1)):
                gots.append([pair(p, *firsts[p])] + ([pair(p, *seconds[p])] if count == 2 else []))
            for s in range(0, tokens, sub):
                rows = pl.ds(s, sub)
                h, g = (sum(product(p, got, rows) for got in gots[p]) for p in range(2))
                if extra:
                    h = h + extra_h[rows, :]
                    g = g + extra_a[rows, :]
                cum = 0.5 * (1.0 + lax.erf(h * root_half))
                act_ref[c, rows, :] = (h * cum).astype(bf)
                slope = cum + h * jnp.exp(-0.5 * h * h) * inv_root_tau
                gh_ref[c, rows, :] = (g * slope).astype(bf)

        for n0 in (1, 2):
            for n1 in (1, 2):
                @pl.when(jnp.logical_not(more) & (two[0] == (n0 == 2)) & (two[1] == (n1 == 2)))
                def _(n0=n0, n1=n1):
                    body(n0, n1, False)

        @pl.when(more)
        def _():
            for p, store in ((0, extra_h), (1, extra_a)):
                store[...] = jnp.zeros_like(store)
                def add(n, p=p, store=store):
                    m = link[p, n]
                    got = pair(p, n, m)
                    for s in range(0, tokens, sub):
                        store[pl.ds(s, sub), :] += product(p, got, pl.ds(s, sub))
                    return link[p, m]
                lax.while_loop(lambda n: n < nb, add, rests[p])
            body(2, 2, True)
        return 0
    lax.fori_loop(0, NCB, column, 0)


def forward(inputs, cotangent, weights, block_rows, block_cols, sub=256):
    T = inputs.shape[0]
    blk = weights.shape[2]
    nb = weights.shape[1]
    smem = pl.BlockSpec(memory_space=pltpu.SMEM)
    hbm = pl.BlockSpec(memory_space=pltpu.HBM)
    vmem = pl.BlockSpec(memory_space=pltpu.VMEM)
    return pl.pallas_call(
        functools.partial(forward_kernel, sub),
        in_specs=[smem, smem, hbm, hbm, hbm],
        out_specs=[vmem] * 4,
        out_shape=[pltpu.VMEM((NCB, T, blk), bf)] * 4,
        scratch_shapes=[
            pltpu.SMEM((2, NCB), jnp.int32), pltpu.SMEM((2, nb + 1), jnp.int32), pltpu.SMEM((2, NCB), jnp.int32),
            pltpu.VMEM(weights.shape, bf), pltpu.VMEM((T, blk), f32), pltpu.VMEM((T, blk), f32), pltpu.SemaphoreType.DMA((2, NCB)),
            pltpu.SemaphoreType.DMA((2,)),
        ],
        compiler_params=pltpu.CompilerParams(vmem_limit_bytes=26 * 2**20),
        name="forward",
    )(block_rows, block_cols, inputs, cotangent, weights)


def combine_kernel(rows_ref, cols_ref, x_v, cot_v, act_v, gh_v, out_ref,
                   psend, own, precv, zsend, mid, fin, vsend, pieces, wide, gsend, grecv,
                   keep_sem, psend_sem, precv_sem, zsend_sem, mid_sem, fin_sem, vsend_sem, vrecv_sem, gsend_sem, grecv_sem):
    MESH = pl.DeviceIdType.MESH
    blk = x_v.shape[2]
    inner = lax.axis_index("inner")
    outer = lax.axis_index("outer")
    z = inner // 2
    core = lax.rem(inner, 2)
    other = 1 - core
    up = {"inner": lax.rem(z + 1, ZS) * 2 + core}
    down = {"inner": lax.rem(z + ZS - 1, ZS) * 2 + core}
    mate = {"inner": z * 2 + other}

    barrier = pltpu.get_barrier_semaphore()
    for peer in (up, down, mate):
        pl.semaphore_signal(barrier, inc=1, device_id=peer, device_id_type=MESH)
    for k in range(1, NOUT):
        pl.semaphore_signal(barrier, inc=1, device_id={"outer": lax.rem(outer + k, NOUT)}, device_id_type=MESH)

    def mate_copy(g):
        return pltpu.make_async_remote_copy(src_ref=psend.at[g], dst_ref=precv.at[g], send_sem=psend_sem.at[g],
                                            recv_sem=precv_sem.at[g], device_id=mate, device_id_type=MESH)

    def z_copy(q, slot):
        dst, sem = ((mid, mid_sem), (mid, mid_sem), (fin, fin_sem), (fin, fin_sem), (fin, fin_sem), (fin, fin_sem))[slot]
        k = (0, 1, 3, 1, 0, 2)[slot]
        peer = up if slot in (0, 2, 4) else down
        return pltpu.make_async_remote_copy(src_ref=zsend.at[q, slot], dst_ref=dst.at[q, k], send_sem=zsend_sem.at[q, slot],
                                            recv_sem=sem.at[q, k], device_id=peer, device_id_type=MESH)

    def grads(q, block0, dst):
        for m in range(OWN):
            n = block0 + m
            r = rows_ref[1 - q, n]
            c = cols_ref[1 - q, n]
            left = act_v[r] if q == 0 else x_v[r]
            right = cot_v[c] if q == 0 else gh_v[c]
            dst[m] = lax.dot_general(left, right, (((0,), (0,)), ((), ())), preferred_element_type=f32).astype(bf)

    HALF = OWN // 2
    def chip(g, lo):
        part = slice(lo, lo + HALF)
        return own[g, part].astype(f32) + precv[g, part].astype(f32)

    def send_z(q, slot, value):
        zsend[q, slot] = value.astype(bf)
        z_copy(q, slot).start()

    def process(q, d):
        g = q * ZS + d
        mate_copy(g).wait_recv()
        if d == 0:
            send_z(q, 0, chip(g, 0))
            send_z(q, 1, chip(g, HALF))
        elif d == 1:
            send_z(q, 2, chip(g, HALF))
        elif d == 2:
            send_z(q, 3, chip(g, 0))
        else:
            z_copy(q, 0).wait_recv()
            send_z(q, 4, chip(q * ZS + 1, 0) + mid[q, 0].astype(f32))
            z_copy(q, 1).wait_recv()
            send_z(q, 5, chip(q * ZS + 2, HALF) + mid[q, 1].astype(f32))

    def v_copy(q, k):
        to = lax.rem(outer + k, NOUT)
        return pltpu.make_async_remote_copy(src_ref=vsend.at[q, to], dst_ref=pieces.at[q, k], send_sem=vsend_sem.at[q, k],
                                            recv_sem=vrecv_sem.at[q, k], device_id={"outer": to}, device_id_type=MESH)

    def finish(q):
        for slot in (2, 3, 4, 5):
            z_copy(q, slot).wait_recv()
        g = q * ZS + 3
        for part in range(2):
            total = chip(g, part * HALF) + fin[q, 2 * part].astype(f32) + fin[q, 2 * part + 1].astype(f32)
            vsend[q, part * (NOUT // 2):(part + 1) * (NOUT // 2)] = total.astype(bf).reshape(NOUT // 2, PIECE, blk)
        for k in range(1, NOUT):
            v_copy(q, k).start()
        keep = pltpu.make_async_copy(vsend.at[q, outer], pieces.at[q, 0], keep_sem.at[q])
        keep.start()

    for q in range(2):
        for d in range(ZS):
            g = q * ZS + d
            owner = lax.rem(z + (2, 1, 3, 0)[d], ZS) * 2
            grads(q, (owner + other) * OWN, psend.at[g])
            if g == 0:
                pl.semaphore_wait(barrier, 3 + NOUT - 1)
            mate_copy(g).start()
            grads(q, (owner + core) * OWN, own.at[g])
            if g > 0:
                process((g - 1) // ZS, (g - 1) % ZS)
    process(1, 3)
    finish(0)
    finish(1)

    def gram(q):
        for k in range(1, NOUT):
            v_copy(q, k).wait_recv()
        pltpu.make_async_copy(vsend.at[q, outer], pieces.at[q, 0], keep_sem.at[q]).wait()
        for s in range(NOUT):
            wide[q, s * PIECE:(s + 1) * PIECE] = pieces[q, lax.rem(outer - s + NOUT, NOUT)].astype(f32)
        picked = [wide[q, pl.ds(r, NOUT, stride=PIECE), :].astype(bf) for r in range(PIECE)]
        flat = jnp.concatenate(picked, axis=1)
        return lax.dot_general(flat, flat, (((1,), (1,)), ((), ())), preferred_element_type=f32)

    g0 = gram(0)
    g1 = gram(1)
    gsend[...] = jnp.concatenate([g0, g1, jnp.zeros((NOUT, blk - 2 * NOUT), f32)], axis=1)

    def g_copy(k):
        to = lax.rem(outer + k, NOUT)
        return pltpu.make_async_remote_copy(src_ref=gsend, dst_ref=grecv.at[k - 1], send_sem=gsend_sem.at[k - 1],
                                            recv_sem=grecv_sem.at[k - 1], device_id={"outer": to}, device_id_type=MESH)
    for k in range(1, NOUT):
        g_copy(k).start()
    total = gsend[...]
    for k in range(1, NOUT):
        g_copy(k).wait_recv()
        total = total + grecv[k - 1]

    row = lax.broadcasted_iota(jnp.int32, (NOUT, NOUT), 0)
    lane = lax.broadcasted_iota(jnp.int32, (NOUT, NOUT), 1)
    for q in range(2):
        q_mat = total[:, q * NOUT:(q + 1) * NOUT]
        coef = jnp.ones((NOUT, 1), f32)
        step = 1
        while step < NOUT:
            same = row == lane
            pair = (row ^ step) == lane
            def mult(axis):
                norm = jnp.maximum(jnp.sum(jnp.where(same, q_mat, 0.0), axis=axis, keepdims=True), 0.0)
                cross = jnp.sum(jnp.where(pair, q_mat, 0.0), axis=axis, keepdims=True)
                return 1.0 - cross / (2.0 * (norm + dot_epsilon))
            mc, mr = mult(1), mult(0)
            coef = coef * mc
            q_mat = q_mat * mc * mr
            def partner(m, axis):
                parts = []
                for i in range(NOUT):
                    j = i ^ step
                    parts.append(m[j:j + 1, :] if axis == 0 else m[:, j:j + 1])
                return jnp.concatenate(parts, axis=axis)
            q_mat = q_mat + partner(q_mat, 0)
            q_mat = q_mat + partner(q_mat, 1)
            step *= 2
        comb = jnp.zeros((PIECE, blk), f32)
        for s in range(NOUT):
            comb = comb + coef[s:s + 1, :] * wide[q, s * PIECE:(s + 1) * PIECE]
        out_ref[1 - q] = comb

    for g in range(2 * ZS):
        mate_copy(g).wait_send()
    for q in range(2):
        for slot in range(6):
            z_copy(q, slot).wait_send()
        for k in range(1, NOUT):
            v_copy(q, k).wait_send()
    for k in range(1, NOUT):
        g_copy(k).wait_send()


def combine(tokens, cots, activated, grad_hidden, block_rows, block_cols):
    blk = tokens.shape[2]
    smem = pl.BlockSpec(memory_space=pltpu.SMEM)
    vmem = pl.BlockSpec(memory_space=pltpu.VMEM)
    dma = pltpu.SemaphoreType.DMA
    V = pltpu.VMEM
    return pl.pallas_call(
        combine_kernel,
        in_specs=[smem, smem, vmem, vmem, vmem, vmem],
        out_specs=vmem,
        out_shape=jax.ShapeDtypeStruct((2, PIECE, blk), f32),
        scratch_shapes=[
            V((2 * ZS, OWN, blk, blk), bf), V((2 * ZS, OWN, blk, blk), bf), V((2 * ZS, OWN, blk, blk), bf),
            V((2, 6, OWN // 2, blk, blk), bf), V((2, 2, OWN // 2, blk, blk), bf), V((2, 4, OWN // 2, blk, blk), bf),
            V((2, NOUT, PIECE, blk), bf), V((2, NOUT, PIECE, blk), bf), V((2, NOUT * PIECE, blk), f32),
            V((NOUT, blk), f32), V((NOUT - 1, NOUT, blk), f32),
            dma((2,)), dma((2 * ZS,)), dma((2 * ZS,)), dma((2, 6)), dma((2, 2)), dma((2, 4)),
            dma((2, NOUT)), dma((2, NOUT)), dma((NOUT - 1,)), dma((NOUT - 1,)),
        ],
        compiler_params=pltpu.CompilerParams(vmem_limit_bytes=16 * 2**20, collective_id=0, has_side_effects=True),
        name="combine",
    )(block_rows, block_cols, tokens, cots, activated, grad_hidden)


def local(inputs, cotangent, weights, block_rows, block_cols, momentum):
    parts = forward(inputs, cotangent, weights, block_rows, block_cols)
    combined = combine(*parts, block_rows, block_cols)
    new_momentum = momentum_decay * momentum + combined
    place = lax.axis_index("inner") * NOUT + lax.axis_index("outer")
    held = lax.dynamic_slice_in_dim(weights.reshape(2, -1, weights.shape[3]), place * PIECE, PIECE, 1)
    new_weights = (held.astype(f32) - step_rate * new_momentum).astype(bf)
    return new_weights, new_momentum


def solution(mesh):
    return jax.shard_map(
        local,
        mesh=mesh,
        in_specs=(
            P(("inner", "outer"), None),
            P(("inner", "outer"), None),
            P(),
            P(),
            P(),
            P(None, ("inner", "outer"), None),
        ),
        out_specs=(P(None, ("inner", "outer"), None), P(None, ("inner", "outer"), None)),
        check_vma=False,
    )
```

```python
import functools
import jax
import jax.numpy as jnp
from jax import lax
from jax.sharding import PartitionSpec as P
from jax.experimental import pallas as pl
from jax.experimental.pallas import tpu as pltpu
f32 = jnp.float32
bf = jnp.bfloat16
i32 = jnp.int32
dot_epsilon = 1e-06
momentum_decay = 0.9
step_rate = 0.05
NCB = 32
OWN = 8
ZS = 4
NOUT = 16
PIECE = 64
root_half = 0.7071067811865476
inv_root_tau = 0.3989422804014327

def forward_kernel(sub, rows_ref, cols_ref, x_hbm, cot_hbm, w_hbm, x_ref, cot_ref, act_ref, gh_ref,
                   head, link, seen, w_ref, extra_h, extra_a, sem, w_sem):
    blk = w_ref.shape[2]
    nb = w_ref.shape[1]
    tokens = x_ref.shape[1]

    w_loads = [pltpu.make_async_copy(w_hbm.at[p], w_ref.at[p], w_sem.at[p]) for p in range(2)]
    for load in w_loads:
        load.start()

    def clear(c, _):
        for p in range(2):
            head[p, c] = nb
            seen[p, c] = 0
        return 0
    lax.fori_loop(0, NCB, clear, 0, unroll=True)
    link[0, nb] = nb
    link[1, nb] = nb

    def push(n, _):
        c = cols_ref[0, n]
        link[0, n] = head[0, c]
        head[0, c] = n
        r = rows_ref[1, n]
        link[1, n] = head[1, r]
        head[1, r] = n
        return 0
    lax.fori_loop(0, nb, push, 0, unroll=8)

    def feature(p, n):
        return rows_ref[0, n] if p == 0 else cols_ref[1, n]

    def copy(p, f):
        src, dst = ((x_hbm, x_ref), (cot_hbm, cot_ref))[p]
        return pltpu.make_async_copy(src.at[:, pl.ds(pl.multiple_of(f * blk, blk), blk)], dst.at[f], sem.at[p, f])

    def fetch(c, _):
        for p in range(2):
            def one(n, p=p):
                f = feature(p, n)
                @pl.when(seen[p, f] == 0)
                def _():
                    seen[p, f] = 1
                    copy(p, f).start()
                return link[p, n]
            lax.while_loop(lambda n: n < nb, one, head[p, c])
        return 0
    lax.fori_loop(0, NCB, fetch, 0)
    for load in w_loads:
        load.wait()

    def arrive(p, f):
        @pl.when(seen[p, f] == 1)
        def _():
            seen[p, f] = 2
            copy(p, f).wait()

    def take(p, n):
        safe = jnp.minimum(n, nb - 1)
        w = w_ref[p, safe]
        return jnp.where(n < nb, w, jnp.zeros_like(w)), feature(p, safe)

    def pair(p, n, m):
        w1, f1 = take(p, n)
        w2, f2 = take(p, m)
        f2 = jnp.where(m < nb, f2, f1)
        return jnp.concatenate([w1, w2], axis=p), f1, f2

    def product(p, got, rows):
        w, f1, f2 = got
        ref = x_ref if p == 0 else cot_ref
        left = jnp.concatenate([ref[f1, rows, :], ref[f2, rows, :]], axis=1)
        return lax.dot_general(left, w, (((1,), (p,)), ((), ())), preferred_element_type=f32)

    def column(c, _):
        firsts, seconds, rests = [], [], []
        for p in range(2):
            def one(n, p=p):
                arrive(p, feature(p, n))
                return link[p, n]
            lax.while_loop(lambda n: n < nb, one, head[p, c])
            a = head[p, c]
            b = link[p, a]
            d = link[p, b]
            e = link[p, d]
            firsts.append((a, b))
            seconds.append((d, e))
            rests.append(link[p, e])
        @pl.when((firsts[0][0] == nb) | (firsts[1][0] == nb))
        def _():
            for p in range(2):
                arrive(p, feature(p, nb - 1))
        more = jnp.logical_or(rests[0] < nb, rests[1] < nb)
        two = [jnp.logical_or(seconds[p][0] < nb, more) for p in range(2)]

        def body(n0, n1, extra):
            gots = []
            for p, count in ((0, n0), (1, n1)):
                gots.append([pair(p, *firsts[p])] + ([pair(p, *seconds[p])] if count == 2 else []))
            for s in range(0, tokens, sub):
                rows = pl.ds(s, sub)
                h, g = (sum(product(p, got, rows) for got in gots[p]) for p in range(2))
                if extra:
                    h = h + extra_h[rows, :]
                    g = g + extra_a[rows, :]
                cum = 0.5 * (1.0 + lax.erf(h * root_half))
                act_ref[c, rows, :] = (h * cum).astype(bf)
                slope = cum + h * jnp.exp(-0.5 * h * h) * inv_root_tau
                gh_ref[c, rows, :] = (g * slope).astype(bf)

        for n0 in (1, 2):
            for n1 in (1, 2):
                @pl.when(jnp.logical_not(more) & (two[0] == (n0 == 2)) & (two[1] == (n1 == 2)))
                def _(n0=n0, n1=n1):
                    body(n0, n1, False)

        @pl.when(more)
        def _():
            for p, store in ((0, extra_h), (1, extra_a)):
                store[...] = jnp.zeros_like(store)
                def add(n, p=p, store=store):
                    m = link[p, n]
                    got = pair(p, n, m)
                    for s in range(0, tokens, sub):
                        store[pl.ds(s, sub), :] += product(p, got, pl.ds(s, sub))
                    return link[p, m]
                lax.while_loop(lambda n: n < nb, add, rests[p])
            body(2, 2, True)
        return 0
    lax.fori_loop(0, NCB, column, 0)


def forward(inputs, cotangent, weights, block_rows, block_cols, sub=256):
    T = inputs.shape[0]
    blk = weights.shape[2]
    nb = weights.shape[1]
    smem = pl.BlockSpec(memory_space=pltpu.SMEM)
    hbm = pl.BlockSpec(memory_space=pltpu.HBM)
    vmem = pl.BlockSpec(memory_space=pltpu.VMEM)
    return pl.pallas_call(
        functools.partial(forward_kernel, sub),
        in_specs=[smem, smem, hbm, hbm, hbm],
        out_specs=[vmem] * 4,
        out_shape=[pltpu.VMEM((NCB, T, blk), bf)] * 4,
        scratch_shapes=[
            pltpu.SMEM((2, NCB), jnp.int32), pltpu.SMEM((2, nb + 1), jnp.int32), pltpu.SMEM((2, NCB), jnp.int32),
            pltpu.VMEM(weights.shape, bf), pltpu.VMEM((T, blk), f32), pltpu.VMEM((T, blk), f32), pltpu.SemaphoreType.DMA((2, NCB)),
            pltpu.SemaphoreType.DMA((2,)),
        ],
        compiler_params=pltpu.CompilerParams(vmem_limit_bytes=20 * 2**20),
        name="forward",
    )(block_rows, block_cols, inputs, cotangent, weights)


def combine_kernel(rows_ref, cols_ref, x_v, cot_v, act_v, gh_v, out_ref,
                   psend, own, precv, zsend, mid, fin, vsend, pieces, wide, gsend, grecv,
                   keep_sem, psend_sem, precv_sem, zsend_sem, mid_sem, fin_sem, vsend_sem, vrecv_sem, gsend_sem, grecv_sem):
    MESH = pl.DeviceIdType.MESH
    blk = x_v.shape[2]
    inner = lax.axis_index("inner")
    outer = lax.axis_index("outer")
    z = inner // 2
    core = lax.rem(inner, 2)
    other = 1 - core
    up = {"inner": lax.rem(z + 1, ZS) * 2 + core}
    down = {"inner": lax.rem(z + ZS - 1, ZS) * 2 + core}
    mate = {"inner": z * 2 + other}

    barrier = pltpu.get_barrier_semaphore()
    for peer in (up, down, mate):
        pl.semaphore_signal(barrier, inc=1, device_id=peer, device_id_type=MESH)
    for k in range(1, NOUT):
        pl.semaphore_signal(barrier, inc=1, device_id={"outer": lax.rem(outer + k, NOUT)}, device_id_type=MESH)

    def mate_copy(g):
        return pltpu.make_async_remote_copy(src_ref=psend.at[g], dst_ref=precv.at[g], send_sem=psend_sem.at[g],
                                            recv_sem=precv_sem.at[g], device_id=mate, device_id_type=MESH)

    def z_copy(q, slot):
        dst, sem = ((mid, mid_sem), (mid, mid_sem), (fin, fin_sem), (fin, fin_sem), (fin, fin_sem), (fin, fin_sem))[slot]
        k = (0, 1, 3, 1, 0, 2)[slot]
        peer = up if slot in (0, 2, 4) else down
        return pltpu.make_async_remote_copy(src_ref=zsend.at[q, slot], dst_ref=dst.at[q, k], send_sem=zsend_sem.at[q, slot],
                                            recv_sem=sem.at[q, k], device_id=peer, device_id_type=MESH)

    def grads(q, block0, dst):
        for m in range(OWN):
            n = block0 + m
            r = rows_ref[1 - q, n]
            c = cols_ref[1 - q, n]
            left = act_v[r] if q == 0 else x_v[r]
            right = cot_v[c] if q == 0 else gh_v[c]
            dst[m] = lax.dot_general(left, right, (((0,), (0,)), ((), ())), preferred_element_type=f32).astype(bf)

    HALF = OWN // 2
    def chip(g, lo):
        part = slice(lo, lo + HALF)
        return own[g, part].astype(f32) + precv[g, part].astype(f32)

    def send_z(q, slot, value):
        zsend[q, slot] = value.astype(bf)
        z_copy(q, slot).start()

    def process(q, d):
        g = q * ZS + d
        mate_copy(g).wait_recv()
        if d == 0:
            send_z(q, 0, chip(g, 0))
            send_z(q, 1, chip(g, HALF))
        elif d == 1:
            send_z(q, 2, chip(g, HALF))
        elif d == 2:
            send_z(q, 3, chip(g, 0))
        else:
            z_copy(q, 0).wait_recv()
            send_z(q, 4, chip(q * ZS + 1, 0) + mid[q, 0].astype(f32))
            z_copy(q, 1).wait_recv()
            send_z(q, 5, chip(q * ZS + 2, HALF) + mid[q, 1].astype(f32))

    def v_copy(q, k):
        to = lax.rem(outer + k, NOUT)
        return pltpu.make_async_remote_copy(src_ref=vsend.at[q, to], dst_ref=pieces.at[q, k], send_sem=vsend_sem.at[q, k],
                                            recv_sem=vrecv_sem.at[q, k], device_id={"outer": to}, device_id_type=MESH)

    def finish(q):
        for slot in (2, 3, 4, 5):
            z_copy(q, slot).wait_recv()
        g = q * ZS + 3
        for part in range(2):
            total = chip(g, part * HALF) + fin[q, 2 * part].astype(f32) + fin[q, 2 * part + 1].astype(f32)
            vsend[q, part * (NOUT // 2):(part + 1) * (NOUT // 2)] = total.astype(bf).reshape(NOUT // 2, PIECE, blk)
        for k in range(1, NOUT):
            v_copy(q, k).start()
        keep = pltpu.make_async_copy(vsend.at[q, outer], pieces.at[q, 0], keep_sem.at[q])
        keep.start()

    for q in range(2):
        for d in range(ZS):
            g = q * ZS + d
            owner = lax.rem(z + (2, 1, 3, 0)[d], ZS) * 2
            grads(q, (owner + other) * OWN, psend.at[g])
            if g == 0:
                pl.semaphore_wait(barrier, 3 + NOUT - 1)
            mate_copy(g).start()
            if g > 0:
                process((g - 1) // ZS, (g - 1) % ZS)
            grads(q, (owner + core) * OWN, own.at[g])
    process(1, 3)
    finish(0)
    finish(1)

    def gram(q):
        for k in range(1, NOUT):
            v_copy(q, k).wait_recv()
        pltpu.make_async_copy(vsend.at[q, outer], pieces.at[q, 0], keep_sem.at[q]).wait()
        for s in range(NOUT):
            wide[q, s * PIECE:(s + 1) * PIECE] = pieces[q, lax.rem(outer - s + NOUT, NOUT)].astype(f32)
        picked = [wide[q, pl.ds(r, NOUT, stride=PIECE), :].astype(bf) for r in range(PIECE)]
        flat = jnp.concatenate(picked, axis=1)
        return lax.dot_general(flat, flat, (((1,), (1,)), ((), ())), preferred_element_type=f32)

    g0 = gram(0)
    g1 = gram(1)
    gsend[...] = jnp.concatenate([g0, g1, jnp.zeros((NOUT, blk - 2 * NOUT), f32)], axis=1)

    def g_copy(k):
        to = lax.rem(outer + k, NOUT)
        return pltpu.make_async_remote_copy(src_ref=gsend, dst_ref=grecv.at[k - 1], send_sem=gsend_sem.at[k - 1],
                                            recv_sem=grecv_sem.at[k - 1], device_id={"outer": to}, device_id_type=MESH)
    for k in range(1, NOUT):
        g_copy(k).start()
    total = gsend[...]
    for k in range(1, NOUT):
        g_copy(k).wait_recv()
        total = total + grecv[k - 1]

    q_mat = jnp.concatenate([total, pltpu.roll(total, blk - NOUT, 1)], axis=0)
    row = lax.broadcasted_iota(jnp.int32, (2 * NOUT, blk), 0)
    lane = lax.broadcasted_iota(jnp.int32, (2 * NOUT, blk), 1)
    place = row % NOUT
    coef = jnp.ones((2 * NOUT, 1), f32)
    step = 1
    while step < NOUT:
        same = place == lane
        pair = (place ^ step) == lane

        def mult(norm, cross):
            return 1.0 - cross / (2.0 * (jnp.maximum(norm, 0.0) + dot_epsilon))
        norms = jnp.where(same, q_mat, 0.0)
        crosses = jnp.where(pair, q_mat, 0.0)
        mc = mult(jnp.sum(norms, axis=1, keepdims=True), jnp.sum(crosses, axis=1, keepdims=True))
        mr = jnp.concatenate([
            jnp.broadcast_to(mult(jnp.sum(norms[h:h + NOUT], axis=0, keepdims=True),
                                  jnp.sum(crosses[h:h + NOUT], axis=0, keepdims=True)), (NOUT, blk))
            for h in (0, NOUT)], axis=0)
        coef = coef * mc
        q_mat = q_mat * mc * mr
        for axis, index in ((0, row), (1, lane)):
            size = q_mat.shape[axis]
            q_mat = q_mat + jnp.where((index & step) > 0, pltpu.roll(q_mat, step, axis), pltpu.roll(q_mat, size - step, axis))
        step *= 2
    for q in range(2):
        comb = jnp.zeros((PIECE, blk), f32)
        for s in range(NOUT):
            comb = comb + coef[q * NOUT + s:q * NOUT + s + 1, :] * wide[q, s * PIECE:(s + 1) * PIECE]
        out_ref[1 - q] = comb

    for g in range(2 * ZS):
        mate_copy(g).wait_send()
    for q in range(2):
        for slot in range(6):
            z_copy(q, slot).wait_send()
        for k in range(1, NOUT):
            v_copy(q, k).wait_send()
    for k in range(1, NOUT):
        g_copy(k).wait_send()


def combine(tokens, cots, activated, grad_hidden, block_rows, block_cols):
    blk = tokens.shape[2]
    smem = pl.BlockSpec(memory_space=pltpu.SMEM)
    vmem = pl.BlockSpec(memory_space=pltpu.VMEM)
    dma = pltpu.SemaphoreType.DMA
    V = pltpu.VMEM
    return pl.pallas_call(
        combine_kernel,
        in_specs=[smem, smem, vmem, vmem, vmem, vmem],
        out_specs=vmem,
        out_shape=jax.ShapeDtypeStruct((2, PIECE, blk), f32),
        scratch_shapes=[
            V((2 * ZS, OWN, blk, blk), bf), V((2 * ZS, OWN, blk, blk), bf), V((2 * ZS, OWN, blk, blk), bf),
            V((2, 6, OWN // 2, blk, blk), bf), V((2, 2, OWN // 2, blk, blk), bf), V((2, 4, OWN // 2, blk, blk), bf),
            V((2, NOUT, PIECE, blk), bf), V((2, NOUT, PIECE, blk), bf), V((2, NOUT * PIECE, blk), f32),
            V((NOUT, blk), f32), V((NOUT - 1, NOUT, blk), f32),
            dma((2,)), dma((2 * ZS,)), dma((2 * ZS,)), dma((2, 6)), dma((2, 2)), dma((2, 4)),
            dma((2, NOUT)), dma((2, NOUT)), dma((NOUT - 1,)), dma((NOUT - 1,)),
        ],
        compiler_params=pltpu.CompilerParams(vmem_limit_bytes=16 * 2**20, collective_id=0, has_side_effects=True),
        name="combine",
    )(block_rows, block_cols, tokens, cots, activated, grad_hidden)


def local(inputs, cotangent, weights, block_rows, block_cols, momentum):
    parts = forward(inputs, cotangent, weights, block_rows, block_cols)
    combined = combine(*parts, block_rows, block_cols)
    new_momentum = momentum_decay * momentum + combined
    place = lax.axis_index("inner") * NOUT + lax.axis_index("outer")
    held = lax.dynamic_slice_in_dim(weights.reshape(2, -1, weights.shape[3]), place * PIECE, PIECE, 1)
    new_weights = (held.astype(f32) - step_rate * new_momentum).astype(bf)
    return new_weights, new_momentum


def solution(mesh):
    return jax.shard_map(
        local,
        mesh=mesh,
        in_specs=(
            P(("inner", "outer"), None),
            P(("inner", "outer"), None),
            P(),
            P(),
            P(),
            P(None, ("inner", "outer"), None),
        ),
        out_specs=(P(None, ("inner", "outer"), None), P(None, ("inner", "outer"), None)),
        check_vma=False,
    )
```
